128 devices in a mesh: row: 16 (over z_hi, y, core), col: 8 (over z_lo, x).
Axes of the slice: x: 4, y: 4, z: 4 (z_hi: 2, z_lo: 2; z = z_hi * 2 + z_lo), core: 2. Of those that a mesh axis runs over, the one named last changes fastest.
Arguments:
- grad_out: bfloat16 [262144, 256], P(('row', 'col')), may hold values from -6 to 6
- preact: bfloat16 [262144, 256], P(('row', 'col')), may hold values from -6 to 6
- features: bfloat16 [262144, 256], P(('col', 'row')), may hold values from -6 to 6
- weight: bfloat16 [256, 256], replicated, may hold values from -0.375 to 0.375
- tiles: bfloat16 [16, 8, 320, 128, 128], P('row', 'col'), may hold values from -0.099609375 to 0.099609375
- tile_rows: int32 [16, 8, 320], P('row', 'col'), may hold values from 0 to 127
- tile_cols: int32 [16, 8, 320], P('row', 'col'), may hold values from 0 to 255
- live_counts: int32 [16, 8], P('row', 'col'), may hold values from 80 to 320, as said below
Outputs:
- grad_features: bfloat16 [262144, 256], P(('col', 'row'))
- grad_weight: float32 [256, 256], replicated
The draws below stay inside these ranges and needn't reach their ends.
Inputs may be any that keep to these rules, and one draw needn't show every extreme that they name: `live_counts`: some block holds exactly 320 live tiles in every draw.
All inputs are finite; a program needn't handle non-finite values.
Results may differ from the reference program's by a relative error of at most 0.02.
Values may be sent and summed in bfloat16 or wider, within the bound.
A program may use at most 192 MiB of HBM per device.

```python
import jax
import jax.numpy as jnp
from jax import lax

F = 256
ND = 2048
KT = 320
TILE = 128
NODES = 262144
RT = 128
CT = 256
N_ROW = 16
N_COL = 8


def draw_live_counts(key, part):
    counts = jax.random.randint(key, (N_ROW * N_COL,), KT // 4, KT + 1)
    chosen = jax.random.randint(jax.random.fold_in(key, 7), (), 0, N_ROW * N_COL)
    counts = counts.at[chosen].set(KT)
    return counts.reshape(N_ROW, N_COL).astype(jnp.int32)


def with_ends(drawn, key, low, top_value):
    longest = drawn.shape.index(max(drawn.shape))
    spots = []
    for shift in (0, 1):
        where = [jax.random.randint(jax.random.fold_in(key, axis), (), 0, length) for axis, length in enumerate(drawn.shape)]
        where[longest] = (where[longest] + shift) % drawn.shape[longest]
        spots.append(tuple(where))
    return drawn.at[spots[0]].set(low).at[spots[1]].set(top_value)


def block_scale(key, dims, split, smallest, high):
    level, own = 1.0, jax.random.fold_in(key, 6)
    for dim, parts in split:
        draws = jnp.exp(jax.random.uniform(jax.random.fold_in(own, dim), (parts,), jnp.float32, smallest / len(split), high / len(split)))
        level = level * jnp.repeat(draws, dims[dim] // parts).reshape([-1 if axis == dim else 1 for axis in range(len(dims))])
    return level


def noise(key, shape, scale, bound, cuts=(), held_as=jnp.bfloat16):
    result = jax.random.normal(key, shape, jnp.float32) * scale
    if len(cuts) > 0:
        result = block_scale(key, shape, cuts, -0.22, 0.18) * result
    return jnp.clip(result, min=-bound, max=bound).astype(held_as)


def setup_inputs(seed: int = 0) -> dict:
    arg_keys = jax.random.split(jax.random.key(seed), 9)
    grad_out = noise(arg_keys[0], (NODES, F), 1.0, 6.0, ((0, 128),))
    preact = noise(arg_keys[1], (NODES, F), 1.0, 6.0, ((0, 128),))
    features = noise(arg_keys[2], (NODES, F), 1.0, 6.0, ((0, 128),))
    weight = noise(arg_keys[3], (F, F), F ** -0.5, 0.375)
    tiles = noise(arg_keys[4], (N_ROW, N_COL, KT, TILE, TILE), 0.018, 0.099609375, ((0, 16), (1, 8)))
    tile_rows = with_ends(jax.random.randint(arg_keys[5], (N_ROW, N_COL, KT), 0, RT), jax.random.fold_in(arg_keys[5], 1), 0, RT - 1).astype(jnp.int32)
    tile_cols = with_ends(jax.random.randint(arg_keys[6], (N_ROW, N_COL, KT), 0, CT), jax.random.fold_in(arg_keys[6], 1), 0, CT - 1).astype(jnp.int32)
    live_counts = draw_live_counts(jax.random.fold_in(arg_keys[8], 71), 0)
    return dict(grad_out=grad_out, preact=preact, features=features, weight=weight, tiles=tiles, tile_rows=tile_rows, tile_cols=tile_cols, live_counts=live_counts)


def reference(grad_out, preact, features, weight, tiles, tile_rows, tile_cols, live_counts):
    masked = jnp.where(preact > 0, grad_out, jnp.zeros_like(grad_out)).astype(jnp.bfloat16)
    row_len = ND * N_COL
    col_len = ND * N_ROW
    accum = jnp.zeros((NODES, F), jnp.float32)

    def one_block(index, accum):
        brow = index // N_COL
        bcol = index % N_COL
        rows_here = lax.dynamic_slice_in_dim(masked, (brow * row_len).astype(jnp.int32), row_len, 0)
        rows_tiled = rows_here.reshape(RT, 128, F)
        tile_blk = tiles[brow, bcol]
        gathered = rows_tiled[tile_rows[brow, bcol]]
        prod = jnp.einsum('kab,kaf->kbf', tile_blk.astype(jnp.float32), gathered.astype(jnp.float32))
        live = jnp.arange(KT, dtype=jnp.int32) < live_counts[brow, bcol]
        prod = jnp.where(live[:, None, None], prod, jnp.zeros_like(prod))
        partial_value = jnp.zeros((CT, 128, F), jnp.float32).at[tile_cols[brow, bcol]].add(prod)
        partial_value = partial_value.reshape(col_len, F).astype(jnp.bfloat16).astype(jnp.float32)
        start = (bcol * col_len).astype(jnp.int32)
        current = lax.dynamic_slice_in_dim(accum, start, col_len, 0)
        return lax.dynamic_update_slice_in_dim(accum, current + partial_value, start, 0)

    accum = lax.fori_loop(0, N_ROW * N_COL, one_block, accum)
    colgrad_b = accum.astype(jnp.bfloat16)
    grad_features = jnp.dot(colgrad_b, weight.T, preferred_element_type=jnp.float32).astype(jnp.bfloat16)
    grad_weight = jnp.dot(features.T, colgrad_b, preferred_element_type=jnp.float32)
    return grad_features, grad_weight
```

```python
import functools

import jax
import jax.numpy as jnp
from jax import lax
from jax.experimental import pallas as pl
from jax.experimental.pallas import tpu as pltpu
from jax.sharding import PartitionSpec as P

MESH = pl.DeviceIdType.MESH
GROUP = 8
STAGE = 16


def block_kernel(rows_ref, cols_ref, count_ref, block_hbm, tiles_hbm, out_hbm,
                 block, acc, tile_buf, stage, block_sem, tile_sem, out_sem):
    slots = tiles_hbm.shape[0]
    groups = slots // GROUP
    depth = tile_buf.shape[0]
    parts = block_sem.shape[0]
    part = block.shape[0] // parts
    count = count_ref[0]
    live_groups = lax.div(count + (GROUP - 1), GROUP)

    def tile_copy(g, slot):
        return pltpu.make_async_copy(
            tiles_hbm.at[pl.ds(g * GROUP, GROUP)], tile_buf.at[slot], tile_sem.at[slot])

    def block_copy(p):
        return pltpu.make_async_copy(
            block_hbm.at[pl.ds(p * part, part)], block.at[pl.ds(p * part, part)], block_sem.at[p])

    for p in range(parts):
        block_copy(p).start()
    for s in range(depth - 1):
        @pl.when(s < live_groups)
        def _():
            tile_copy(s, s).start()

    zero = jnp.zeros(acc.shape[1:], jnp.float32)

    def clear(i, carry):
        acc[i] = zero
        return carry

    lax.fori_loop(0, acc.shape[0], clear, 0)
    for p in range(parts):
        block_copy(p).wait()

    def step(g, carry):
        slot = lax.rem(g, depth)
        ahead = g + depth - 1

        @pl.when(ahead < live_groups)
        def _():
            tile_copy(ahead, lax.rem(ahead, depth)).start()

        tile_copy(g, slot).wait()
        prods = []
        for u in range(GROUP):
            k = g * GROUP + u
            tile = tile_buf[slot, u]
            vals = block[rows_ref[k]]
            prods.append(lax.dot_general(
                tile, vals, (((0,), (0,)), ((), ())), preferred_element_type=jnp.float32))
        for u in range(GROUP):
            k = g * GROUP + u
            c = cols_ref[k]
            keep = jnp.where(k < count, 1.0, 0.0).astype(jnp.float32)
            acc[c] = acc[c] + prods[u] * keep
        return carry

    lax.fori_loop(0, live_groups, step, 0)

    pieces = acc.shape[0] // STAGE

    def out_copy(i, slot):
        return pltpu.make_async_copy(
            stage.at[slot], out_hbm.at[pl.ds(i * STAGE, STAGE)], out_sem.at[slot])

    def emit(i, carry):
        slot = lax.rem(i, 2)

        @pl.when(i >= 2)
        def _():
            out_copy(i - 2, slot).wait()

        for u in range(STAGE):
            stage[slot, u] = acc[i * STAGE + u].astype(jnp.bfloat16)
        out_copy(i, slot).start()
        return carry

    lax.fori_loop(0, pieces, emit, 0)
    out_copy(pieces - 2, lax.rem(pieces - 2, 2)).wait()
    out_copy(pieces - 1, lax.rem(pieces - 1, 2)).wait()


def block_product(block, tiles, rows, cols, count, col_tiles):
    row_tiles, side, width = block.shape
    slots = tiles.shape[0]
    return pl.pallas_call(
        block_kernel,
        name="block_product",
        grid_spec=pltpu.PrefetchScalarGridSpec(
            num_scalar_prefetch=3,
            grid=(1,),
            in_specs=[pl.BlockSpec(memory_space=pl.ANY)] * 2,
            out_specs=pl.BlockSpec(memory_space=pl.ANY),
            scratch_shapes=[
                pltpu.VMEM((row_tiles, side, width), jnp.bfloat16),
                pltpu.VMEM((col_tiles, side, width), jnp.float32),
                pltpu.VMEM((6, GROUP, side, side), jnp.bfloat16),
                pltpu.VMEM((2, STAGE, side, width), jnp.bfloat16),
                pltpu.SemaphoreType.DMA((4,)),
                pltpu.SemaphoreType.DMA((6,)),
                pltpu.SemaphoreType.DMA((2,)),
            ],
        ),
        out_shape=jax.ShapeDtypeStruct((col_tiles, side, width), jnp.bfloat16),
        compiler_params=pltpu.CompilerParams(
            dimension_semantics=("arbitrary",), vmem_limit_bytes=56 * 1024 * 1024),
        cost_estimate=pl.CostEstimate(
            flops=2 * slots * side * side * width, transcendentals=0,
            bytes_accessed=2 * (block.size + tiles.size + col_tiles * side * width)),
    )(rows, cols, count, block, tiles)


def place():
    r, q = lax.axis_index("row"), lax.axis_index("col")
    core, y, z_hi = lax.rem(r, 2), lax.rem(lax.div(r, 2), 4), lax.div(r, 8)
    x, z_lo = lax.rem(q, 4), lax.div(q, 4)
    return core, x, y, z_hi, z_lo


def device(core, x, y, z_hi, z_lo):
    return ((z_hi * 4 + y) * 2 + core, z_lo * 4 + x)


def meet(partners):
    barrier = pltpu.get_barrier_semaphore()
    for partner in partners:
        pl.semaphore_signal(barrier, inc=1, device_id=partner, device_id_type=MESH)
    pl.semaphore_wait(barrier, len(partners))


def gather_kernel(grad_ref, preact_ref, out_hbm, masked, local_sem, send_sem, recv_sem):
    core, x, y, z_hi, z_lo = place()
    tiles = masked.shape[0]
    half = tiles // 2
    right = device(core, lax.rem(x + 1, 4), y, z_hi, z_lo)
    left = device(core, lax.rem(x + 3, 4), y, z_hi, z_lo)
    over = device(core, x, y, z_hi, 1 - z_lo)

    def rows(z_at, x_at, part):
        return pl.ds((z_at * 4 + x_at) * tiles + part * half, half)

    grads = grad_ref[...]
    masked[...] = jnp.where(preact_ref[...] > 0, grads, jnp.zeros_like(grads))
    meet([right, left, over])

    def send(n, source, z_at, x_at, part, target):
        spot = rows(z_at, x_at, part)
        copy = pltpu.make_async_remote_copy(
            src_ref=masked.at[pl.ds(part * half, half)] if source is None else out_hbm.at[spot],
            dst_ref=out_hbm.at[spot], send_sem=send_sem.at[n], recv_sem=recv_sem.at[n],
            device_id=target, device_id_type=MESH)
        copy.start()
        return copy

    x_r, x_l, x_o = lax.rem(x + 1, 4), lax.rem(x + 3, 4), lax.rem(x + 2, 4)
    other = 1 - z_lo
    copies = {}
    copies[0] = send(0, None, z_lo, x, 0, right)
    copies[1] = send(1, None, z_lo, x, 1, left)
    copies[2] = send(2, None, z_lo, x, 0, over)
    copies[3] = send(3, None, z_lo, x, 1, over)
    copies[4] = send(4, None, z_lo, x, 1, right)
    copies[5] = send(5, None, z_lo, x, 0, left)
    own = pltpu.make_async_copy(
        masked, out_hbm.at[pl.ds((z_lo * 4 + x) * tiles, tiles)], local_sem)
    own.start()
    copies[0].wait_recv()
    copies[6] = send(6, 1, z_lo, x_l, 0, right)
    copies[1].wait_recv()
    copies[7] = send(7, 1, z_lo, x_r, 1, left)
    copies[2].wait_recv()
    copies[8] = send(8, 1, other, x, 0, right)
    copies[9] = send(9, 1, other, x, 0, left)
    copies[3].wait_recv()
    copies[10] = send(10, 1, other, x, 1, right)
    copies[11] = send(11, 1, other, x, 1, left)
    copies[6].wait_recv()
    copies[12] = send(12, 1, z_lo, x_o, 0, over)
    copies[7].wait_recv()
    copies[13] = send(13, 1, z_lo, x_o, 1, over)
    for n in (4, 5, 8, 9, 10, 11, 12, 13):
        copies[n].wait_recv()
    for n in range(14):
        copies[n].wait_send()
    own.wait()


def gather_rows(grad_out, preact, members):
    tiles, side, width = grad_out.shape
    return pl.pallas_call(
        gather_kernel,
        name="gather_rows",
        in_specs=[pl.BlockSpec(memory_space=pltpu.VMEM)] * 2,
        out_specs=pl.BlockSpec(memory_space=pl.ANY),
        out_shape=jax.ShapeDtypeStruct((members * tiles, side, width), jnp.bfloat16),
        scratch_shapes=[
            pltpu.VMEM((tiles, side, width), jnp.bfloat16),
            pltpu.SemaphoreType.DMA,
            pltpu.SemaphoreType.DMA((14,)),
            pltpu.SemaphoreType.DMA((14,)),
        ],
        compiler_params=pltpu.CompilerParams(
            collective_id=1, has_side_effects=True, vmem_limit_bytes=60 * 1024 * 1024),
    )(grad_out, preact)


ORDER = tuple((s, d) for s in (0, 1) for d in (2, 1, 3, 0))


def reduce_kernel(part_hbm, features_ref, weight_ref, grad_ref, gw_ref,
                  own, core_in, far_l, far_r, near_l, near_r, relay, cross,
                  term, core_half, plane_in, z_in, halves,
                  load_sem, send_sem, recv_sem, ar_send, ar_recv):
    core, x, y, z_hi, z_lo = place()
    tiles = own.shape[1]
    half = tiles // 2
    z = z_hi * 2 + z_lo

    def at_z(zz):
        return device(core, x, y, lax.div(zz, 2), lax.rem(zz, 2))

    mate = device(1 - core, x, y, z_hi, z_lo)
    right = device(core, x, lax.rem(y + 1, 4), z_hi, z_lo)
    left = device(core, x, lax.rem(y + 3, 4), z_hi, z_lo)
    above, below = at_z(lax.rem(z + 1, 4)), at_z(lax.rem(z + 3, 4))
    plane = [device(core, lax.rem(x + d % 4, 4), lax.rem(y + d // 4, 4), z_hi, z_lo)
             for d in range(1, 16)]
    column = [at_z(lax.rem(z + d, 4)) for d in range(1, 4)]

    def chunk(s, d, c):
        z_to = 1 - z_hi if s == 0 else z_hi
        return pl.ds(((z_to * 4 + lax.rem(y + d, 4)) * 2 + c) * tiles, tiles)

    loads = [pltpu.make_async_copy(part_hbm.at[chunk(s, d, core)], own.at[s * 4 + d], load_sem.at[n])
             for n, (s, d) in enumerate(ORDER)]
    for load in loads[:4]:
        load.start()
    meet([mate] + plane + column)

    def remote(n, source, target_ref, target):
        return pltpu.make_async_remote_copy(
            src_ref=source, dst_ref=target_ref, send_sem=send_sem.at[n], recv_sem=recv_sem.at[n],
            device_id=target, device_id_type=MESH)

    swaps = [remote(n, part_hbm.at[chunk(s, d, 1 - core)], core_in.at[s * 4 + d], mate)
             for n, (s, d) in enumerate(ORDER)]
    ahead = 3
    for swap in swaps[:ahead]:
        swap.start()

    def add_into(dst, dst_at, src, src_at, count):
        def one(t, carry):
            dst[dst_at[0], dst_at[1] + t] = (
                dst[dst_at[0], dst_at[1] + t].astype(jnp.float32)
                + src[src_at[0], src_at[1] + t].astype(jnp.float32)).astype(jnp.bfloat16)
            return carry
        lax.fori_loop(0, count, one, 0)

    def settle(n):
        s, d = ORDER[n]
        if n + ahead < len(ORDER):
            swaps[n + ahead].start()
        if n + 4 < len(ORDER):
            loads[n + 4].start()
        loads[n].wait()
        swaps[n].wait_recv()
        add_into(own, (s * 4 + d, 0), core_in, (s * 4 + d, 0), tiles)

    low, high = pl.ds(0, half), pl.ds(half, half)
    sent = list(swaps)

    def go(n, source, target_ref, target):
        copy = remote(n, source, target_ref, target)
        copy.start()
        sent.append(copy)
        return copy

    far, direct, merged = {}, {}, {}

    def spread(s):
        first = s * 4
        base = 8 + s * 6
        settle(first)
        far[s] = (go(base, own.at[s * 4 + 2, low], far_l.at[s], right),
                  go(base + 1, own.at[s * 4 + 2, high], far_r.at[s], left))
        settle(first + 1)
        one = go(base + 2, own.at[s * 4 + 1, high], near_l.at[s, high], right)
        settle(first + 2)
        two = go(base + 3, own.at[s * 4 + 3, low], near_r.at[s, low], left)
        direct[s] = (one, two)
        settle(first + 3)

    def forward(s):
        base = 8 + s * 6
        far[s][0].wait_recv()
        add_into(own, (s * 4 + 1, 0), far_l, (s, 0), half)
        one = go(base + 4, own.at[s * 4 + 1, low], near_l.at[s, low], right)
        far[s][1].wait_recv()
        add_into(own, (s * 4 + 3, half), far_r, (s, 0), half)
        two = go(base + 5, own.at[s * 4 + 3, high], near_r.at[s, high], left)
        merged[s] = (one, two)

    spread(0)
    forward(0)
    spread(1)

    def three(t):
        return (own[0, t].astype(jnp.float32) + near_l[0, t].astype(jnp.float32)
                + near_r[0, t].astype(jnp.float32)).astype(jnp.bfloat16)

    def close(start):
        def one(t, carry):
            own[0, start + t] = three(start + t)
            return carry
        lax.fori_loop(0, half, one, 0)

    merged[0][0].wait_recv()
    direct[0][1].wait_recv()
    close(0)
    up = go(20, own.at[0, low], relay.at[0], above)
    merged[0][1].wait_recv()
    direct[0][0].wait_recv()
    close(half)
    down = go(21, own.at[0, high], relay.at[1], below)
    forward(1)
    up.wait_recv()
    up_end = go(22, relay.at[0], cross.at[0], above)
    down.wait_recv()
    down_end = go(23, relay.at[1], cross.at[1], below)

    term[...] = jnp.zeros_like(term)
    pair = 4

    def finish(part):
        def one(g, carry):
            t = part * half + g * pair
            spot = pl.ds(t, pair)
            total = (own[4, spot].astype(jnp.float32) + near_l[1, spot].astype(jnp.float32)
                     + near_r[1, spot].astype(jnp.float32)
                     + cross[part, pl.ds(g * pair, pair)].astype(jnp.float32))
            summed = total.astype(jnp.bfloat16).reshape(pair * total.shape[1], total.shape[2])
            grads = lax.dot_general(summed, weight_ref[...], (((1,), (1,)), ((), ())),
                                    preferred_element_type=jnp.float32)
            grad_ref[spot] = grads.astype(jnp.bfloat16).reshape(total.shape)
            feats = features_ref[spot].reshape(summed.shape)
            term[...] += lax.dot_general(feats, summed, (((0,), (0,)), ((), ())),
                                         preferred_element_type=jnp.float32)
            return carry
        lax.fori_loop(0, half // pair, one, 0)

    merged[1][0].wait_recv()
    direct[1][1].wait_recv()
    up_end.wait_recv()
    finish(0)
    merged[1][1].wait_recv()
    direct[1][0].wait_recv()
    down_end.wait_recv()
    finish(1)

    def tiny(n, source, target_ref, target):
        copy = pltpu.make_async_remote_copy(
            src_ref=source, dst_ref=target_ref, send_sem=ar_send.at[n], recv_sem=ar_recv.at[n],
            device_id=target, device_id_type=MESH)
        copy.start()
        sent.append(copy)
        return copy

    lines = core_half.shape[0]
    piece = lines // 16
    spot = y * 4 + x

    def piece_of(p):
        return pl.ds(pl.multiple_of(p * piece, piece), piece)

    def side_of(c):
        return pl.ds(pl.multiple_of(c * lines, lines), lines)

    swap = tiny(0, term.at[side_of(1 - core)], core_half, mate)
    swap.wait_recv()
    halves[...] = term[side_of(core), :] + core_half[...]
    spots = [lax.rem(y + d // 4, 4) * 4 + lax.rem(x + d % 4, 4) for d in range(1, 16)]
    out = [tiny(d, halves.at[piece_of(spots[d - 1])], plane_in.at[d - 1], plane[d - 1])
           for d in range(1, 16)]
    total = halves[piece_of(spot), :]
    for d in range(1, 16):
        out[d - 1].wait_recv()
        total = total + plane_in[d - 1]
    z_in[z] = total
    ups = [tiny(15 + d, z_in.at[z], z_in.at[z], column[d - 1]) for d in range(1, 4)]
    for copy in ups:
        copy.wait_recv()
    total = (z_in[0] + z_in[1]) + (z_in[2] + z_in[3])
    mine = pl.ds(pl.multiple_of(core * lines + spot * piece, piece), piece)
    gw_ref[mine, :] = total
    out = [tiny(18 + d, gw_ref.at[mine], gw_ref.at[mine], plane[d - 1]) for d in range(1, 16)]
    for copy in out:
        copy.wait_recv()
    swap = tiny(34, gw_ref.at[side_of(core)], gw_ref.at[side_of(core)], mate)
    swap.wait_recv()
    for copy in sent:
        copy.wait_send()


def reduce_finish(partial_value, features, weight):
    tiles, side, width = features.shape
    depth = weight.shape[0]
    block = (tiles, side, width)
    half = (tiles // 2, side, width)
    return pl.pallas_call(
        reduce_kernel,
        name="reduce_finish",
        in_specs=[pl.BlockSpec(memory_space=pl.ANY)] + [pl.BlockSpec(memory_space=pltpu.VMEM)] * 2,
        out_specs=[pl.BlockSpec(memory_space=pltpu.VMEM)] * 2,
        out_shape=[jax.ShapeDtypeStruct(block, jnp.bfloat16),
                   jax.ShapeDtypeStruct((depth, width), jnp.float32)],
        scratch_shapes=[
            pltpu.VMEM((8,) + block, jnp.bfloat16),
            pltpu.VMEM((8,) + block, jnp.bfloat16),
            pltpu.VMEM((2,) + half, jnp.bfloat16),
            pltpu.VMEM((2,) + half, jnp.bfloat16),
            pltpu.VMEM((2,) + block, jnp.bfloat16),
            pltpu.VMEM((2,) + block, jnp.bfloat16),
            pltpu.VMEM((2,) + half, jnp.bfloat16),
            pltpu.VMEM((2,) + half, jnp.bfloat16),
            pltpu.VMEM((depth, width), jnp.float32),
            pltpu.VMEM((depth // 2, width), jnp.float32),
            pltpu.VMEM((15, depth // 32, width), jnp.float32),
            pltpu.VMEM((4, depth // 32, width), jnp.float32),
            pltpu.VMEM((depth // 2, width), jnp.float32),
            pltpu.SemaphoreType.DMA((8,)),
            pltpu.SemaphoreType.DMA((24,)),
            pltpu.SemaphoreType.DMA((24,)),
            pltpu.SemaphoreType.DMA((35,)),
            pltpu.SemaphoreType.DMA((35,)),
        ],
        compiler_params=pltpu.CompilerParams(
            collective_id=0, has_side_effects=True, vmem_limit_bytes=60 * 1024 * 1024),
    )(partial_value, features, weight)


def body(grad_out, preact, features, weight, tiles, tile_rows, tile_cols, live_counts):
    nodes, width = grad_out.shape
    side = tiles.shape[-1]
    slots = tiles.shape[2]
    shape = (nodes // side, side, width)
    block = gather_rows(grad_out.reshape(shape), preact.reshape(shape), lax.axis_size("col"))
    col_tiles = lax.axis_size("row") * nodes // side
    partial_value = block_product(
        block, tiles.reshape(slots, side, side),
        tile_rows.reshape(slots), tile_cols.reshape(slots), live_counts.reshape(1), col_tiles)
    grad_features, grad_weight = reduce_finish(partial_value, features.reshape(shape), weight)
    return (grad_features.reshape(nodes, width), grad_weight)


def solution(mesh):
    in_specs = (
        P(("row", "col"), None),
        P(("row", "col"), None),
        P(("col", "row"), None),
        P(),
        P("row", "col", None, None, None),
        P("row", "col", None),
        P("row", "col", None),
        P("row", "col"),
    )
    out_specs = (P(("col", "row"), None), P())
    return jax.shard_map(body, mesh=mesh, in_specs=in_specs, out_specs=out_specs, check_vma=False)
```

```python
import math

import jax
import jax.numpy as jnp
from jax import lax
from jax.experimental import pallas as pl
from jax.experimental.pallas import tpu as pltpu
from jax.sharding import PartitionSpec as P

MESH = pl.DeviceIdType.MESH
GROUP = 8
LANES = 128
ORDER = tuple((s, d) for s in (0, 1) for d in (2, 1, 3, 0))
GATHER, REDUCE, SUM = 14, 24, 35


def place():
    r, q = lax.axis_index("row"), lax.axis_index("col")
    core, y, z_hi = lax.rem(r, 2), lax.rem(lax.div(r, 2), 4), lax.div(r, 8)
    x, z_lo = lax.rem(q, 4), lax.div(q, 4)
    return core, x, y, z_hi, z_lo


def device(core, x, y, z_hi, z_lo):
    return ((z_hi * 4 + y) * 2 + core, z_lo * 4 + x)


def meet(partners):
    barrier = pltpu.get_barrier_semaphore()
    for partner in partners:
        pl.semaphore_signal(barrier, inc=1, device_id=partner, device_id_type=MESH)
    pl.semaphore_wait(barrier, len(partners))


def layer_kernel(order_ref, last_ref, grad_hbm, preact_hbm, features_hbm, weight_ref, tiles_hbm,
                 grad_out_hbm, gw_ref,
                 tiles, block_0, block_1, runs, mate_part, own, core_in, far_l, far_r, near_l, near_r,
                 relay, cross, features, grads, term, core_half, plane_in, z_in, halves,
                 load_sem, send_sem, recv_sem):
    core, x, y, z_hi, z_lo = place()
    block = (block_0, block_1)
    count = own.shape[1]
    half = count // 2
    slots = tiles.shape[0]
    row_bits = int(math.log2(block_0.shape[0]))
    z = z_hi * 2 + z_lo
    x_r, x_l, x_o = lax.rem(x + 1, 4), lax.rem(x + 3, 4), lax.rem(x + 2, 4)

    def at_z(zz):
        return device(core, x, y, lax.div(zz, 2), lax.rem(zz, 2))

    mate = device(1 - core, x, y, z_hi, z_lo)
    x_right, x_left = device(core, x_r, y, z_hi, z_lo), device(core, x_l, y, z_hi, z_lo)
    over = device(core, x, y, z_hi, 1 - z_lo)
    y_right = device(core, x, lax.rem(y + 1, 4), z_hi, z_lo)
    y_left = device(core, x, lax.rem(y + 3, 4), z_hi, z_lo)
    above, below = at_z(lax.rem(z + 1, 4)), at_z(lax.rem(z + 3, 4))
    plane = [device(core, lax.rem(x + d % 4, 4), lax.rem(y + d // 4, 4), z_hi, z_lo)
             for d in range(1, 16)]
    column = [at_z(lax.rem(z + d, 4)) for d in range(1, 4)]
    sent, done = [], []

    def go(n, source, target_ref, target):
        copy = pltpu.make_async_remote_copy(
            src_ref=source, dst_ref=target_ref, send_sem=send_sem.at[n], recv_sem=recv_sem.at[n],
            device_id=target, device_id_type=MESH)
        copy.start()
        sent.append(copy)
        return copy

    def fetch(n, source, target_ref):
        copy = pltpu.make_async_copy(source, target_ref, load_sem.at[n])
        copy.start()
        return copy

    stages = []
    for h in range(2):
        lanes = pl.ds(h * LANES, LANES)
        stages.append((
            fetch(2 * h, grad_hbm.at[:, :, lanes], runs.at[pl.ds(2 * h * count, count)]),
            fetch(2 * h + 1, preact_hbm.at[:, :, lanes], runs.at[pl.ds((2 * h + 1) * count, count)])))
    quarter = slots // 4
    tile_loads = [fetch(4 + p, tiles_hbm.at[pl.ds(p * quarter, quarter)], tiles.at[pl.ds(p * quarter, quarter)])
                  for p in range(4)]
    feature_load = fetch(8, features_hbm, features)
    mine = (z_lo * 4 + x) * count

    def mask(h):
        for load in stages[h]:
            load.wait()

        def one(t, carry):
            g = runs[2 * h * count + t]
            keep = runs[(2 * h + 1) * count + t].astype(jnp.float32) > 0
            block[h][mine + t] = jnp.where(keep, g.astype(jnp.float32), 0.0).astype(jnp.bfloat16)
            return carry
        lax.fori_loop(0, count, one, 0)

    mask(0)
    meet([mate] + plane + column)

    gathers = ({}, {})

    def pass_on(h, n, z_at, x_at, part, target):
        spot = block[h].at[pl.ds((z_at * 4 + x_at) * count + part * half, half)]
        gathers[h][n] = go(h * GATHER + n, spot, spot, target)

    def gather_first(h):
        pass_on(h, 0, z_lo, x, 0, x_right)
        pass_on(h, 1, z_lo, x, 1, x_left)
        pass_on(h, 2, z_lo, x, 0, over)
        pass_on(h, 4, z_lo, x, 1, x_right)
        pass_on(h, 5, z_lo, x, 0, x_left)
        pass_on(h, 3, z_lo, x, 1, over)

    def gather_second(h):
        gathers[h][0].wait_recv()
        pass_on(h, 6, z_lo, x_l, 0, x_right)
        gathers[h][1].wait_recv()
        pass_on(h, 7, z_lo, x_r, 1, x_left)
        gathers[h][2].wait_recv()
        pass_on(h, 8, 1 - z_lo, x, 0, x_right)
        pass_on(h, 9, 1 - z_lo, x, 0, x_left)
        gathers[h][3].wait_recv()
        pass_on(h, 10, 1 - z_lo, x, 1, x_right)
        pass_on(h, 11, 1 - z_lo, x, 1, x_left)

    def gather_third(h):
        gathers[h][6].wait_recv()
        pass_on(h, 12, z_lo, x_o, 0, over)
        gathers[h][7].wait_recv()
        pass_on(h, 13, z_lo, x_o, 1, over)

    def gather_rest(h):
        for n in (4, 5, 8, 9, 10, 11, 12, 13):
            gathers[h][n].wait_recv()

    def turn(p):
        tile_loads[p].wait()

        def one(i, carry):
            for u in range(4):
                k = p * quarter + i * 4 + u
                tiles[k] = tiles[k].T
            return carry
        lax.fori_loop(0, quarter // 4, one, 0)

    def multiply(h, start, stop, acc):
        def one(g, acc):
            prods, keeps = [], []
            for u in range(GROUP):
                entry = order_ref[g * GROUP + u]
                keeps.append((entry & 1) > 0)
                row = (entry >> 1) & (block_0.shape[0] - 1)
                prods.append(jnp.dot(tiles[entry >> (row_bits + 1)], block[h][row],
                                     preferred_element_type=jnp.float32))
            for u in range(GROUP):
                acc = jnp.where(keeps[u], acc, 0.0) + prods[u]
                runs[g * GROUP + u] = acc.astype(jnp.bfloat16)
            return acc
        return lax.fori_loop(start // GROUP, stop // GROUP, one, acc)

    def chunk(s, d, c):
        z_to = 1 - z_hi if s == 0 else z_hi
        return ((z_to * 4 + lax.rem(y + d, 4)) * 2 + c) * count

    def column_total(c):
        entry = last_ref[c]
        return runs[entry >> 1].astype(jnp.float32) * (entry & 1).astype(jnp.float32)

    swaps = ({}, {})

    def swap(h, n):
        s, d = ORDER[n]
        base = chunk(s, d, 1 - core)

        def one(t, carry):
            mate_part[n, t] = column_total(base + t).astype(jnp.bfloat16)
            return carry
        if h == 1:
            swaps[0][n].wait_send()
            done.append(swaps[0][n])
        lax.fori_loop(0, count, one, 0)
        swaps[h][n] = go(2 * GATHER + h * REDUCE + n, mate_part.at[n], core_in.at[h * 8 + s * 4 + d], mate)

    def settle(h, n):
        if n == 0:
            for m in range(3):
                swap(h, m)
        if n + 3 < len(ORDER):
            swap(h, n + 3)
        s, d = ORDER[n]
        base = chunk(s, d, core)
        at = h * 8 + s * 4 + d
        swaps[h][n].wait_recv()

        def one(t, carry):
            own[at, t] = (column_total(base + t) + core_in[at, t].astype(jnp.float32)).astype(jnp.bfloat16)
            return carry
        lax.fori_loop(0, count, one, 0)

    low, high = pl.ds(0, half), pl.ds(half, half)
    far, direct, merged, hops = {}, {}, {}, {}

    def spread(h, s):
        first, at, b = s * 4, h * 8 + s * 4, h * 2 + s
        base = 2 * GATHER + h * REDUCE + 8 + s * 6
        settle(h, first)
        far[b] = (go(base, own.at[at + 2, low], far_l.at[b], y_right),
                  go(base + 1, own.at[at + 2, high], far_r.at[b], y_left))
        settle(h, first + 1)
        one = go(base + 2, own.at[at + 1, high], near_l.at[b, high], y_right)
        settle(h, first + 2)
        two = go(base + 3, own.at[at + 3, low], near_r.at[b, low], y_left)
        direct[b] = (one, two)
        settle(h, first + 3)

    def add_far(at, start, src, b):
        def one(t, carry):
            own[at, start + t] = (own[at, start + t].astype(jnp.float32)
                                  + src[b, t].astype(jnp.float32)).astype(jnp.bfloat16)
            return carry
        lax.fori_loop(0, half, one, 0)

    def forward(h, s):
        at, b = h * 8 + s * 4, h * 2 + s
        base = 2 * GATHER + h * REDUCE + 8 + s * 6
        far[b][0].wait_recv()
        add_far(at + 1, 0, far_l, b)
        one = go(base + 4, own.at[at + 1, low], near_l.at[b, low], y_right)
        far[b][1].wait_recv()
        add_far(at + 3, half, far_r, b)
        two = go(base + 5, own.at[at + 3, high], near_r.at[b, high], y_left)
        merged[b] = (one, two)

    def near_sum(at, b, t):
        return (own[at, t].astype(jnp.float32) + near_l[b, t].astype(jnp.float32)
                + near_r[b, t].astype(jnp.float32))

    def near_wait(b, part):
        merged[b][part].wait_recv()
        direct[b][1 - part].wait_recv()

    def close(h):
        at, b = h * 8, h * 2
        base = 2 * GATHER + h * REDUCE + 20
        for part in range(2):
            near_wait(b, part)

            def one(t, carry):
                tt = part * half + t
                own[at, tt] = near_sum(at, b, tt).astype(jnp.bfloat16)
                return carry
            lax.fori_loop(0, half, one, 0)
            hops[h, part] = go(base + part, own.at[at, low if part == 0 else high],
                               relay.at[h * 2 + part], above if part == 0 else below)

    def onward(h):
        base = 2 * GATHER + h * REDUCE + 22
        for part in range(2):
            hops[h, part].wait_recv()
            hops[h, 2 + part] = go(base + part, relay.at[h * 2 + part], cross.at[h * 2 + part],
                                   above if part == 0 else below)

    pair = 4

    def total_of(h):
        at, b = h * 8 + 4, h * 2 + 1
        for part in range(2):
            near_wait(b, part)
            hops[h, 2 + part].wait_recv()

            def one(g, acc):
                t = part * half + g * pair
                spot = pl.ds(t, pair)
                summed = (near_sum(at, b, spot)
                          + cross[h * 2 + part, pl.ds(g * pair, pair)].astype(jnp.float32)).astype(jnp.bfloat16)
                own[at, spot] = summed
                summed = summed.reshape(pair * LANES, LANES)
                if h == 1:
                    before = own[4, spot].reshape(pair * LANES, LANES)
                    both = jnp.concatenate([before, summed], axis=1)
                    out = lax.dot_general(both, weight_ref[...], (((1,), (1,)), ((), ())),
                                          preferred_element_type=jnp.float32)
                    grads[spot] = out.astype(jnp.bfloat16).reshape((pair,) + grads.shape[1:])
                feats = features[spot].reshape(pair * LANES, features.shape[2])
                return acc + lax.dot_general(feats, summed, (((0,), (0,)), ((), ())),
                                             preferred_element_type=jnp.float32)
            acc = lax.fori_loop(0, half // pair, one, jnp.zeros((term.shape[0], LANES), jnp.float32))
            if part == 0:
                term[:, h * LANES:(h + 1) * LANES] = acc
            else:
                term[:, h * LANES:(h + 1) * LANES] += acc

    nothing = jnp.zeros((LANES, LANES), jnp.float32)
    middle = slots // 2 // GROUP * GROUP
    gather_first(0)
    mask(1)
    turn(0)
    gather_second(0)
    turn(1)
    turn(2)
    gather_third(0)
    gather_first(1)
    turn(3)
    gather_rest(0)
    acc = multiply(0, 0, middle, nothing)
    gather_second(1)
    multiply(0, middle, slots, acc)
    spread(0, 0)
    gather_third(1)
    forward(0, 0)
    spread(0, 1)
    gather_rest(1)
    acc = multiply(1, 0, middle, nothing)
    close(0)
    multiply(1, middle, slots, acc)
    forward(0, 1)
    spread(1, 0)
    onward(0)
    forward(1, 0)
    spread(1, 1)
    feature_load.wait()
    total_of(0)
    close(1)
    forward(1, 1)
    onward(1)
    total_of(1)
    store = fetch(9, grads, grad_out_hbm)

    first = 2 * GATHER + 2 * REDUCE
    lines = core_half.shape[0]
    piece = lines // 16
    spot = y * 4 + x

    def piece_of(p):
        return pl.ds(pl.multiple_of(p * piece, piece), piece)

    def side_of(c):
        return pl.ds(pl.multiple_of(c * lines, lines), lines)

    trade = go(first, term.at[side_of(1 - core)], core_half, mate)
    trade.wait_recv()
    halves[...] = term[side_of(core), :] + core_half[...]
    spots = [lax.rem(y + d // 4, 4) * 4 + lax.rem(x + d % 4, 4) for d in range(1, 16)]
    out = [go(first + d, halves.at[piece_of(spots[d - 1])], plane_in.at[d - 1], plane[d - 1])
           for d in range(1, 16)]
    total = halves[piece_of(spot), :]
    for d in range(1, 16):
        out[d - 1].wait_recv()
        total = total + plane_in[d - 1]
    z_in[z] = total
    ups = [go(first + 15 + d, z_in.at[z], z_in.at[z], column[d - 1]) for d in range(1, 4)]
    for copy in ups:
        copy.wait_recv()
    total = (z_in[0] + z_in[1]) + (z_in[2] + z_in[3])
    part = pl.ds(pl.multiple_of(core * lines + spot * piece, piece), piece)
    gw_ref[part, :] = total
    out = [go(first + 18 + d, gw_ref.at[part], gw_ref.at[part], plane[d - 1]) for d in range(1, 16)]
    for copy in out:
        copy.wait_recv()
    trade = go(first + 34, gw_ref.at[side_of(core)], gw_ref.at[side_of(core)], mate)
    trade.wait_recv()
    store.wait()
    for copy in sent:
        if not any(copy is one for one in done):
            copy.wait_send()


def layer_backward(order, last, grad_out, preact, features, weight, tiles, members):
    count, side, width = grad_out.shape
    depth = weight.shape[0]
    slots = tiles.shape[0]
    piece = (side, LANES)
    full, part = (count,) + piece, (count // 2,) + piece
    n_sems = 2 * GATHER + 2 * REDUCE + SUM

    def bf16(*shape):
        return pltpu.VMEM(shape, jnp.bfloat16)

    def f32(*shape):
        return pltpu.VMEM(shape, jnp.float32)

    return pl.pallas_call(
        layer_kernel,
        name="layer_backward",
        in_specs=[pl.BlockSpec(memory_space=pltpu.SMEM)] * 2
        + [pl.BlockSpec(memory_space=pl.ANY)] * 3
        + [pl.BlockSpec(memory_space=pltpu.VMEM), pl.BlockSpec(memory_space=pl.ANY)],
        out_specs=[pl.BlockSpec(memory_space=pl.ANY), pl.BlockSpec(memory_space=pltpu.VMEM)],
        out_shape=[jax.ShapeDtypeStruct((count, side, width), jnp.bfloat16),
                   jax.ShapeDtypeStruct((depth, width), jnp.float32)],
        scratch_shapes=[
            bf16(slots, *piece),
            bf16(members * count, *piece),
            bf16(members * count, *piece),
            bf16(slots, *piece),
            bf16(8, *full),
            bf16(16, *full),
            bf16(16, *full),
            bf16(4, *part),
            bf16(4, *part),
            bf16(4, *full),
            bf16(4, *full),
            bf16(4, *part),
            bf16(4, *part),
            bf16(count, side, width),
            bf16(count, side, width),
            f32(depth, width),
            f32(depth // 2, width),
            f32(15, depth // 32, width),
            f32(4, depth // 32, width),
            f32(depth // 2, width),
            pltpu.SemaphoreType.DMA((10,)),
            pltpu.SemaphoreType.DMA((n_sems,)),
            pltpu.SemaphoreType.DMA((n_sems,)),
        ],
        compiler_params=pltpu.CompilerParams(
            collective_id=0, has_side_effects=True, vmem_limit_bytes=63 * 1024 * 1024),
    )(order, last, grad_out, preact, features, weight, tiles)


def slot_tables(rows, cols, live_count, row_tiles, col_tiles):
    slots = rows.shape[0]
    k = lax.iota(jnp.int32, slots)
    live = k < live_count
    col = jnp.where(live, cols, col_tiles)
    key = col * slots + k
    rank = jnp.sum((key[None, :] < key[:, None]).astype(jnp.int32), axis=1)
    same = (col[None, :] == col[:, None]) & (k[None, :] < k[:, None])
    again = jnp.max(same.astype(jnp.int32), axis=1)
    packed = (k * row_tiles + rows) * 2 + again
    order = jnp.sum(jnp.where(rank[None, :] == k[:, None], packed[None, :], 0), axis=1)
    c = lax.iota(jnp.int32, col_tiles)
    upto = jnp.sum((col[None, :] <= c[:, None]).astype(jnp.int32), axis=1)
    here = jnp.max((col[None, :] == c[:, None]).astype(jnp.int32), axis=1)
    last = jnp.maximum(upto - 1, 0) * 2 + here
    return order, last


def body(grad_out, preact, features, weight, tiles, tile_rows, tile_cols, live_counts):
    nodes, width = grad_out.shape
    side = tiles.shape[-1]
    slots = tiles.shape[2]
    shape = (nodes // side, side, width)
    members = lax.axis_size("col")
    col_tiles = lax.axis_size("row") * nodes // side
    order, last = slot_tables(
        tile_rows.reshape(slots), tile_cols.reshape(slots), live_counts.reshape(()),
        members * nodes // side, col_tiles)
    grad_features, grad_weight = layer_backward(
        order, last, grad_out.reshape(shape), preact.reshape(shape), features.reshape(shape), weight,
        tiles.reshape(slots, side, side), members)
    return (grad_features.reshape(nodes, width), grad_weight)


def solution(mesh):
    in_specs = (
        P(("row", "col"), None),
        P(("row", "col"), None),
        P(("col", "row"), None),
        P(),
        P("row", "col", None, None, None),
        P("row", "col", None),
        P("row", "col", None),
        P("row", "col"),
    )
    out_specs = (P(("col", "row"), None), P())
    return jax.shard_map(body, mesh=mesh, in_specs=in_specs, out_specs=out_specs, check_vma=False)
```

```python
import math

import jax
import jax.numpy as jnp
from jax import lax
from jax.experimental import pallas as pl
from jax.experimental.pallas import tpu as pltpu
from jax.sharding import PartitionSpec as P

MESH = pl.DeviceIdType.MESH
GROUP = 16
LANES = 128
ORDER = tuple((s, d) for s in (0, 1) for d in (2, 1, 3, 0))
GATHER, REDUCE, SUM = 14, 34, 35
FIRST = (2, 6)


def place():
    r, q = lax.axis_index("row"), lax.axis_index("col")
    core, y, z_hi = lax.rem(r, 2), lax.rem(lax.div(r, 2), 4), lax.div(r, 8)
    x, z_lo = lax.rem(q, 4), lax.div(q, 4)
    return core, x, y, z_hi, z_lo


def device(core, x, y, z_hi, z_lo):
    return ((z_hi * 4 + y) * 2 + core, z_lo * 4 + x)


def meet(partners):
    barrier = pltpu.get_barrier_semaphore()
    for partner in partners:
        pl.semaphore_signal(barrier, inc=1, device_id=partner, device_id_type=MESH)
    pl.semaphore_wait(barrier, len(partners))


def layer_kernel(order_ref, last_ref, grad_hbm, preact_hbm, features_hbm, weight_ref, tiles_hbm,
                 grad_out_hbm, gw_ref,
                 tiles, block_0, block_1, runs, mate_part, own, core_in, far_l, far_r, near_l, near_r,
                 relay, cross, early_0, early_1, early_in_0, early_in_1, features, terms, term, core_half, plane_in, z_in, halves,
                 load_sem, send_sem, recv_sem):
    core, x, y, z_hi, z_lo = place()
    block = (block_0, block_1)
    count = own.shape[1]
    half = count // 2
    slots = tiles.shape[0]
    row_bits = int(math.log2(block_0.shape[0]))
    z = z_hi * 2 + z_lo
    x_r, x_l, x_o = lax.rem(x + 1, 4), lax.rem(x + 3, 4), lax.rem(x + 2, 4)

    def at_z(zz):
        return device(core, x, y, lax.div(zz, 2), lax.rem(zz, 2))

    mate = device(1 - core, x, y, z_hi, z_lo)
    x_right, x_left = device(core, x_r, y, z_hi, z_lo), device(core, x_l, y, z_hi, z_lo)
    over = device(core, x, y, z_hi, 1 - z_lo)
    y_right = device(core, x, lax.rem(y + 1, 4), z_hi, z_lo)
    y_left = device(core, x, lax.rem(y + 3, 4), z_hi, z_lo)
    above, below = at_z(lax.rem(z + 1, 4)), at_z(lax.rem(z + 3, 4))
    plane = [device(core, lax.rem(x + d % 4, 4), lax.rem(y + d // 4, 4), z_hi, z_lo)
             for d in range(1, 16)]
    column = [at_z(lax.rem(z + d, 4)) for d in range(1, 4)]
    sent, done = [], []
    early, early_in = (early_0, early_1), (early_in_0, early_in_1)

    def go(n, source, target_ref, target):
        copy = pltpu.make_async_remote_copy(
            src_ref=source, dst_ref=target_ref, send_sem=send_sem.at[n], recv_sem=recv_sem.at[n],
            device_id=target, device_id_type=MESH)
        copy.start()
        sent.append(copy)
        return copy

    def fetch(n, source, target_ref):
        copy = pltpu.make_async_copy(source, target_ref, load_sem.at[n])
        copy.start()
        return copy

    stages = []
    for h in range(2):
        lanes = pl.ds(h * LANES, LANES)
        stages.append((
            fetch(2 * h, grad_hbm.at[:, :, lanes], runs.at[pl.ds(2 * h * count, count)]),
            fetch(2 * h + 1, preact_hbm.at[:, :, lanes], runs.at[pl.ds((2 * h + 1) * count, count)])))
    quarter = slots // 4
    tile_loads = [fetch(4 + p, tiles_hbm.at[pl.ds(p * quarter, quarter)], tiles.at[pl.ds(p * quarter, quarter)])
                  for p in range(4)]
    feature_load = fetch(8, features_hbm, features)
    mine = (z_lo * 4 + x) * count

    def mask(h):
        for load in stages[h]:
            load.wait()

        def one(t, carry):
            g = runs[2 * h * count + t]
            keep = runs[(2 * h + 1) * count + t].astype(jnp.float32) > 0
            block[h][mine + t] = jnp.where(keep, g.astype(jnp.float32), 0.0).astype(jnp.bfloat16)
            return carry
        lax.fori_loop(0, count, one, 0)

    meet([mate] + plane + column)
    mask(0)

    gathers = ({}, {})

    def pass_on(h, n, z_at, x_at, part, target):
        spot = block[h].at[pl.ds((z_at * 4 + x_at) * count + part * half, half)]
        gathers[h][n] = go(h * GATHER + n, spot, spot, target)

    def gather_first(h):
        pass_on(h, 0, z_lo, x, 0, x_right)
        pass_on(h, 1, z_lo, x, 1, x_left)
        pass_on(h, 2, z_lo, x, 0, over)
        pass_on(h, 4, z_lo, x, 1, x_right)
        pass_on(h, 5, z_lo, x, 0, x_left)
        pass_on(h, 3, z_lo, x, 1, over)

    def gather_second(h):
        gathers[h][0].wait_recv()
        pass_on(h, 6, z_lo, x_l, 0, x_right)
        gathers[h][1].wait_recv()
        pass_on(h, 7, z_lo, x_r, 1, x_left)
        gathers[h][2].wait_recv()
        pass_on(h, 8, 1 - z_lo, x, 0, x_right)
        pass_on(h, 9, 1 - z_lo, x, 0, x_left)
        gathers[h][3].wait_recv()
        pass_on(h, 10, 1 - z_lo, x, 1, x_right)
        pass_on(h, 11, 1 - z_lo, x, 1, x_left)

    def gather_third(h):
        gathers[h][6].wait_recv()
        pass_on(h, 12, z_lo, x_o, 0, over)
        gathers[h][7].wait_recv()
        pass_on(h, 13, z_lo, x_o, 1, over)

    def gather_rest(h):
        for n in (4, 5, 8, 9, 10, 11, 12, 13):
            gathers[h][n].wait_recv()

    def turn(p):
        tile_loads[p].wait()

        def one(i, carry):
            for u in range(8):
                k = p * quarter + i * 8 + u
                tiles[k] = tiles[k].T
            return carry
        lax.fori_loop(0, quarter // 8, one, 0)

    def multiply(h, start, stop, acc):
        def one(g, acc):
            prods, keeps = [], []
            for u in range(GROUP):
                entry = order_ref[g * GROUP + u]
                keeps.append((entry & 1) > 0)
                row = (entry >> 1) & (block_0.shape[0] - 1)
                prods.append(jnp.dot(tiles[entry >> (row_bits + 1)], block[h][row],
                                     preferred_element_type=jnp.float32))
            for u in range(GROUP):
                acc = jnp.where(keeps[u], acc, 0.0) + prods[u]
                runs[g * GROUP + u] = acc.astype(jnp.bfloat16)
            return acc
        return lax.fori_loop(start // GROUP, stop // GROUP, one, acc)

    def chunk(s, d, c):
        z_to = 1 - z_hi if s == 0 else z_hi
        return ((z_to * 4 + lax.rem(y + d, 4)) * 2 + c) * count

    zero = jnp.zeros((LANES, LANES), jnp.bfloat16)
    swaps = ({}, {})

    def swap(h, n):
        s, d = ORDER[n]
        base = chunk(s, d, 1 - core)

        def one(g, carry):
            for u in range(8):
                t = g * 8 + u
                entry = last_ref[base + t]
                mate_part[n, t] = jnp.where((entry & 1) > 0, runs[entry >> 1], zero)
            return carry
        if h == 1:
            swaps[0][n].wait_send()
            done.append(swaps[0][n])
        lax.fori_loop(0, count // 8, one, 0)
        swaps[h][n] = go(2 * GATHER + h * REDUCE + n, mate_part.at[n], core_in.at[h * 8 + s * 4 + d], mate)

    def settle(h, n):
        if n == 0:
            for m in range(3):
                swap(h, m)
        if n + 3 < len(ORDER):
            swap(h, n + 3)
        s, d = ORDER[n]
        base = chunk(s, d, core)
        at = h * 8 + s * 4 + d
        swaps[h][n].wait_recv()

        def one(g, carry):
            for u in range(8):
                t = g * 8 + u
                entry = last_ref[base + t]
                mine_here = jnp.where((entry & 1) > 0, runs[entry >> 1], zero).astype(jnp.float32)
                own[at, t] = (mine_here + core_in[at, t].astype(jnp.float32)).astype(jnp.bfloat16)
            return carry
        lax.fori_loop(0, count // 8, one, 0)

    far, direct, merged, hops = {}, {}, {}, {}

    def base_of(h):
        return 2 * GATHER + h * REDUCE + 8

    def segment(h, g):
        rest = count - FIRST[h]
        s, start, length = ((0, 0, rest), (1, 0, rest), (1, rest, FIRST[h]))[g]
        return s, start, length // 2, h * 8 + s * 4, h * 2 + s

    def spread(h, g):
        s, start, size, at, b = segment(h, g)
        base = base_of(h) + g * 6
        low, high = pl.ds(start, size), pl.ds(start + size, size)
        spot = pl.ds(start // 2, size)
        if g < 2:
            settle(h, s * 4)
        far[h, g] = (go(base, own.at[at + 2, low], far_l.at[b, spot], y_right),
                     go(base + 1, own.at[at + 2, high], far_r.at[b, spot], y_left))
        if g < 2:
            settle(h, s * 4 + 1)
        one = go(base + 2, own.at[at + 1, high], near_l.at[b, high], y_right)
        if g < 2:
            settle(h, s * 4 + 2)
        two = go(base + 3, own.at[at + 3, low], near_r.at[b, low], y_left)
        direct[h, g] = (one, two)
        if g < 2:
            settle(h, s * 4 + 3)

    def add_far(at, start, size, src, b, spot):
        for t in range(size):
            own[at, start + t] = (own[at, start + t].astype(jnp.float32)
                                  + src[b, spot + t].astype(jnp.float32)).astype(jnp.bfloat16)

    def forward(h, g):
        s, start, size, at, b = segment(h, g)
        base = base_of(h) + g * 6
        low, high = pl.ds(start, size), pl.ds(start + size, size)
        far[h, g][0].wait_recv()
        add_far(at + 1, start, size, far_l, b, start // 2)
        one = go(base + 4, own.at[at + 1, low], near_l.at[b, low], y_right)
        far[h, g][1].wait_recv()
        add_far(at + 3, start + size, size, far_r, b, start // 2)
        two = go(base + 5, own.at[at + 3, high], near_r.at[b, high], y_left)
        merged[h, g] = (one, two)

    def near_sum(at, b, t):
        return (own[at, t].astype(jnp.float32) + near_l[b, t].astype(jnp.float32)
                + near_r[b, t].astype(jnp.float32))

    def near_wait(h, g, part):
        merged[h, g][part].wait_recv()
        direct[h, g][1 - part].wait_recv()

    def early_send(h):
        size = FIRST[h] // 2
        for part in range(2):
            rows = pl.ds(count - FIRST[h] + part * size, size)
            hops[h, 4 + part] = go(base_of(h) + 22 + part, own.at[pl.ds(h * 8, 4), rows],
                                   early[h].at[part], below if part else above)

    def early_hop(h):
        for part in range(2):
            hops[h, 4 + part].wait_recv()
            hops[h, 6 + part] = go(base_of(h) + 24 + part, early[h].at[part],
                                   early_in[h].at[part], below if part else above)

    def early_add(h):
        size = FIRST[h] // 2
        for part in range(2):
            hops[h, 6 + part].wait_recv()
            for d in range(4):
                for t in range(size):
                    tt = count - FIRST[h] + part * size + t
                    own[h * 8 + 4 + d, tt] = (
                        own[h * 8 + 4 + d, tt].astype(jnp.float32)
                        + early_in[h][part, d, t].astype(jnp.float32)).astype(jnp.bfloat16)

    def close(h):
        s, start, size, at, b = segment(h, 0)
        for part in range(2):
            near_wait(h, 0, part)

            for t in range(part * size, (part + 1) * size):
                own[at, t] = near_sum(at, b, t).astype(jnp.bfloat16)
            hops[h, part] = go(base_of(h) + 18 + part, own.at[at, pl.ds(part * size, size)],
                               relay.at[h * 2 + part, pl.ds(0, size)], below if part else above)

    def onward(h):
        size = segment(h, 0)[2]
        for part in range(2):
            hops[h, part].wait_recv()
            spot = pl.ds(0, size)
            hops[h, 2 + part] = go(base_of(h) + 20 + part, relay.at[h * 2 + part, spot],
                                   cross.at[h * 2 + part, spot], below if part else above)

    def total_of(h, g):
        s, start, size, at, b = segment(h, g)
        for part in range(2):
            near_wait(h, g, part)
            spot = pl.ds(start + part * size, size)
            total = near_sum(at, b, spot)
            if g == 1:
                hops[h, 2 + part].wait_recv()
                total = total + cross[h * 2 + part, pl.ds(0, size)].astype(jnp.float32)
            summed = total.astype(jnp.bfloat16)
            own[at, spot] = summed
            feats = features[spot].reshape(size * LANES, features.shape[2])
            more = lax.dot_general(feats, summed.reshape(size * LANES, LANES), (((0,), (0,)), ((), ())),
                                   preferred_element_type=jnp.float32)
            column = slice(h * LANES, (h + 1) * LANES)
            held = terms if g == 1 else term
            if part == 0:
                held[:, column] = more
            else:
                held[:, column] += more

    pair = 4

    def feature_grads():
        def one(g, carry):
            spot = pl.ds(g * pair, pair)
            both = jnp.concatenate([own[4, spot].reshape(pair * LANES, LANES),
                                    own[12, spot].reshape(pair * LANES, LANES)], axis=1)
            out = lax.dot_general(both, weight_ref[...], (((1,), (1,)), ((), ())),
                                  preferred_element_type=jnp.float32)
            features[spot] = out.astype(jnp.bfloat16).reshape((pair,) + features.shape[1:])
            return carry
        lax.fori_loop(0, count // pair, one, 0)
        return fetch(9, features, grad_out_hbm)

    nothing = jnp.zeros((LANES, LANES), jnp.float32)
    middle = slots // 2 // GROUP * GROUP
    gather_first(0)
    mask(1)
    turn(0)
    gather_second(0)
    turn(1)
    turn(2)
    gather_third(0)
    gather_first(1)
    turn(3)
    gather_rest(0)
    acc = multiply(0, 0, middle, nothing)
    gather_second(1)
    multiply(0, middle, slots, acc)
    spread(0, 0)
    early_send(0)
    early_hop(0)
    gather_third(1)
    forward(0, 0)
    spread(0, 1)
    early_add(0)
    spread(0, 2)
    gather_rest(1)
    close(0)
    forward(0, 1)
    multiply(1, 0, slots, nothing)
    onward(0)
    spread(1, 0)
    early_send(1)
    forward(0, 2)
    forward(1, 0)
    spread(1, 1)
    early_hop(1)
    feature_load.wait()
    total_of(0, 2)
    close(1)
    total_of(0, 1)
    forward(1, 1)
    early_add(1)
    spread(1, 2)
    onward(1)
    forward(1, 2)
    total_of(1, 1)
    total_of(1, 2)
    term[...] = terms[...] + term[...]

    first = 2 * GATHER + 2 * REDUCE
    lines = core_half.shape[0]
    piece = lines // 16
    spot = y * 4 + x

    def piece_of(p):
        return pl.ds(pl.multiple_of(p * piece, piece), piece)

    def side_of(c):
        return pl.ds(pl.multiple_of(c * lines, lines), lines)

    trade = go(first, term.at[side_of(1 - core)], core_half, mate)
    store = feature_grads()
    trade.wait_recv()
    halves[...] = term[side_of(core), :] + core_half[...]
    spots = [lax.rem(y + d // 4, 4) * 4 + lax.rem(x + d % 4, 4) for d in range(1, 16)]
    out = [go(first + d, halves.at[piece_of(spots[d - 1])], plane_in.at[d - 1], plane[d - 1])
           for d in range(1, 16)]
    total = halves[piece_of(spot), :]
    for d in range(1, 16):
        out[d - 1].wait_recv()
        total = total + plane_in[d - 1]
    z_in[z] = total
    ups = [go(first + 15 + d, z_in.at[z], z_in.at[z], column[d - 1]) for d in range(1, 4)]
    for copy in ups:
        copy.wait_recv()
    total = (z_in[0] + z_in[1]) + (z_in[2] + z_in[3])
    part = pl.ds(pl.multiple_of(core * lines + spot * piece, piece), piece)
    gw_ref[part, :] = total
    out = [go(first + 18 + d, gw_ref.at[part], gw_ref.at[part], plane[d - 1]) for d in range(1, 16)]
    for copy in out:
        copy.wait_recv()
    trade = go(first + 34, gw_ref.at[side_of(core)], gw_ref.at[side_of(core)], mate)
    trade.wait_recv()
    store.wait()
    for copy in sent:
        if not any(copy is one for one in done):
            copy.wait_send()


def layer_backward(order, last, grad_out, preact, features, weight, tiles, members):
    count, side, width = grad_out.shape
    depth = weight.shape[0]
    slots = tiles.shape[0]
    piece = (side, LANES)
    full, part = (count,) + piece, (count // 2,) + piece
    n_sems = 2 * GATHER + 2 * REDUCE + SUM

    def bf16(*shape):
        return pltpu.VMEM(shape, jnp.bfloat16)

    def f32(*shape):
        return pltpu.VMEM(shape, jnp.float32)

    return pl.pallas_call(
        layer_kernel,
        name="layer_backward",
        in_specs=[pl.BlockSpec(memory_space=pltpu.SMEM)] * 2
        + [pl.BlockSpec(memory_space=pl.ANY)] * 3
        + [pl.BlockSpec(memory_space=pltpu.VMEM), pl.BlockSpec(memory_space=pl.ANY)],
        out_specs=[pl.BlockSpec(memory_space=pl.ANY), pl.BlockSpec(memory_space=pltpu.VMEM)],
        out_shape=[jax.ShapeDtypeStruct((count, side, width), jnp.bfloat16),
                   jax.ShapeDtypeStruct((depth, width), jnp.float32)],
        scratch_shapes=[
            bf16(slots, *piece),
            bf16(members * count, *piece),
            bf16(members * count, *piece),
            bf16(slots, *piece),
            bf16(8, *full),
            bf16(16, *full),
            bf16(16, *full),
            bf16(4, *part),
            bf16(4, *part),
            bf16(4, *full),
            bf16(4, *full),
            bf16(4, *part),
            bf16(4, *part),
            *[bf16(2, 4, rows // 2, *piece) for rows in FIRST * 2],
            bf16(count, side, width),
            f32(depth, width),
            f32(depth, width),
            f32(depth // 2, width),
            f32(15, depth // 32, width),
            f32(4, depth // 32, width),
            f32(depth // 2, width),
            pltpu.SemaphoreType.DMA((10,)),
            pltpu.SemaphoreType.DMA((n_sems,)),
            pltpu.SemaphoreType.DMA((n_sems,)),
        ],
        compiler_params=pltpu.CompilerParams(
            collective_id=0, has_side_effects=True, vmem_limit_bytes=63 * 1024 * 1024),
    )(order, last, grad_out, preact, features, weight, tiles)


def slot_tables(rows, cols, live_count, row_tiles, col_tiles):
    slots = rows.shape[0]
    k = lax.iota(jnp.int32, slots)
    live = k < live_count
    col = jnp.where(live, cols, col_tiles)
    key = col * slots + k
    rank = jnp.sum((key[None, :] < key[:, None]).astype(jnp.int32), axis=1)
    same = (col[None, :] == col[:, None]) & (k[None, :] < k[:, None])
    again = jnp.max(same.astype(jnp.int32), axis=1)
    packed = (k * row_tiles + rows) * 2 + again
    order = jnp.sum(jnp.where(rank[None, :] == k[:, None], packed[None, :], 0), axis=1)
    c = lax.iota(jnp.int32, col_tiles)
    upto = jnp.sum((col[None, :] <= c[:, None]).astype(jnp.int32), axis=1)
    here = jnp.max((col[None, :] == c[:, None]).astype(jnp.int32), axis=1)
    last = jnp.maximum(upto - 1, 0) * 2 + here
    return order, last


def body(grad_out, preact, features, weight, tiles, tile_rows, tile_cols, live_counts):
    nodes, width = grad_out.shape
    side = tiles.shape[-1]
    slots = tiles.shape[2]
    shape = (nodes // side, side, width)
    members = lax.axis_size("col")
    col_tiles = lax.axis_size("row") * nodes // side
    order, last = slot_tables(
        tile_rows.reshape(slots), tile_cols.reshape(slots), live_counts.reshape(()),
        members * nodes // side, col_tiles)
    grad_features, grad_weight = layer_backward(
        order, last, grad_out.reshape(shape), preact.reshape(shape), features.reshape(shape), weight,
        tiles.reshape(slots, side, side), members)
    return (grad_features.reshape(nodes, width), grad_weight)


def solution(mesh):
    in_specs = (
        P(("row", "col"), None),
        P(("row", "col"), None),
        P(("col", "row"), None),
        P(),
        P("row", "col", None, None, None),
        P("row", "col", None),
        P("row", "col", None),
        P("row", "col"),
    )
    out_specs = (P(("col", "row"), None), P())
    return jax.shard_map(body, mesh=mesh, in_specs=in_specs, out_specs=out_specs, check_vma=False)
```

```python
import math

import jax
import jax.numpy as jnp
from jax import lax
from jax.experimental import pallas as pl
from jax.experimental.pallas import tpu as pltpu
from jax.sharding import PartitionSpec as P

MESH = pl.DeviceIdType.MESH
GROUP = 32
LANES = 128
ORDER = tuple((s, d) for s in (0, 1) for d in (2, 1, 3, 0))
GATHER, REDUCE, SUM = 14, 34, 38
FIRST = (2, 6)


def place():
    r, q = lax.axis_index("row"), lax.axis_index("col")
    core, y, z_hi = lax.rem(r, 2), lax.rem(lax.div(r, 2), 4), lax.div(r, 8)
    x, z_lo = lax.rem(q, 4), lax.div(q, 4)
    return core, x, y, z_hi, z_lo


def device(core, x, y, z_hi, z_lo):
    return ((z_hi * 4 + y) * 2 + core, z_lo * 4 + x)


def meet(partners):
    barrier = pltpu.get_barrier_semaphore()
    for partner in partners:
        pl.semaphore_signal(barrier, inc=1, device_id=partner, device_id_type=MESH)
    pl.semaphore_wait(barrier, len(partners))


def layer_kernel(order_ref, last_ref, grad_hbm, preact_hbm, features_hbm, weight_ref, tiles_hbm,
                 grad_out_hbm, gw_ref,
                 tiles, block_0, block_1, runs, mate_part, own, core_in, far_l, far_r, near_l, near_r,
                 relay, cross, early_0, early_1, early_in_0, early_in_1, features, terms, term, plane_in, z_in,
                 load_sem, send_sem, recv_sem):
    core, x, y, z_hi, z_lo = place()
    block = (block_0, block_1)
    count = own.shape[1]
    half = count // 2
    slots = tiles.shape[0]
    row_bits = int(math.log2(block_0.shape[0]))
    z = z_hi * 2 + z_lo
    x_r, x_l, x_o = lax.rem(x + 1, 4), lax.rem(x + 3, 4), lax.rem(x + 2, 4)

    def at_z(zz):
        return device(core, x, y, lax.div(zz, 2), lax.rem(zz, 2))

    mate = device(1 - core, x, y, z_hi, z_lo)
    x_right, x_left = device(core, x_r, y, z_hi, z_lo), device(core, x_l, y, z_hi, z_lo)
    over = device(core, x, y, z_hi, 1 - z_lo)
    y_right = device(core, x, lax.rem(y + 1, 4), z_hi, z_lo)
    y_left = device(core, x, lax.rem(y + 3, 4), z_hi, z_lo)
    above, below = at_z(lax.rem(z + 1, 4)), at_z(lax.rem(z + 3, 4))
    plane = [device(core, lax.rem(x + d % 4, 4), lax.rem(y + d // 4, 4), z_hi, z_lo)
             for d in range(1, 16)]
    column = [device(core if d % 2 == 0 else 1 - core, x, y,
                     lax.div(lax.rem(z + d // 2, 4), 2), lax.rem(lax.rem(z + d // 2, 4), 2))
              for d in range(1, 8)]
    sent, done = [], []
    early, early_in = (early_0, early_1), (early_in_0, early_in_1)

    def go(n, source, target_ref, target):
        copy = pltpu.make_async_remote_copy(
            src_ref=source, dst_ref=target_ref, send_sem=send_sem.at[n], recv_sem=recv_sem.at[n],
            device_id=target, device_id_type=MESH)
        copy.start()
        sent.append(copy)
        return copy

    def fetch(n, source, target_ref):
        copy = pltpu.make_async_copy(source, target_ref, load_sem.at[n])
        copy.start()
        return copy

    stages = []
    for h in range(2):
        lanes = pl.ds(h * LANES, LANES)
        stages.append((
            fetch(2 * h, grad_hbm.at[:, :, lanes], runs.at[pl.ds(2 * h * count, count)]),
            fetch(2 * h + 1, preact_hbm.at[:, :, lanes], runs.at[pl.ds((2 * h + 1) * count, count)])))
    quarter = slots // 4
    tile_loads = [fetch(4 + p, tiles_hbm.at[pl.ds(p * quarter, quarter)], tiles.at[pl.ds(p * quarter, quarter)])
                  for p in range(4)]
    feature_load = fetch(8, features_hbm, features)
    mine = (z_lo * 4 + x) * count

    def mask(h):
        for load in stages[h]:
            load.wait()

        def one(t, carry):
            g = runs[2 * h * count + t]
            keep = runs[(2 * h + 1) * count + t].astype(jnp.float32) > 0
            block[h][mine + t] = jnp.where(keep, g.astype(jnp.float32), 0.0).astype(jnp.bfloat16)
            return carry
        lax.fori_loop(0, count, one, 0)

    meet(plane + column)
    mask(0)

    gathers = ({}, {})

    def pass_on(h, n, z_at, x_at, part, target):
        spot = block[h].at[pl.ds((z_at * 4 + x_at) * count + part * half, half)]
        gathers[h][n] = go(h * GATHER + n, spot, spot, target)

    def gather_over(h):
        pass_on(h, 2, z_lo, x, 0, over)
        pass_on(h, 3, z_lo, x, 1, over)

    def gather_ring(h):
        pass_on(h, 0, z_lo, x, 0, x_right)
        pass_on(h, 1, z_lo, x, 1, x_left)
        pass_on(h, 4, z_lo, x, 1, x_right)
        pass_on(h, 5, z_lo, x, 0, x_left)

    def gather_second(h):
        gathers[h][0].wait_recv()
        pass_on(h, 6, z_lo, x_l, 0, x_right)
        gathers[h][1].wait_recv()
        pass_on(h, 7, z_lo, x_r, 1, x_left)
        gathers[h][2].wait_recv()
        pass_on(h, 8, 1 - z_lo, x, 0, x_right)
        pass_on(h, 9, 1 - z_lo, x, 0, x_left)
        gathers[h][3].wait_recv()
        pass_on(h, 10, 1 - z_lo, x, 1, x_right)
        pass_on(h, 11, 1 - z_lo, x, 1, x_left)

    def gather_third(h):
        gathers[h][6].wait_recv()
        pass_on(h, 12, z_lo, x_o, 0, over)
        gathers[h][7].wait_recv()
        pass_on(h, 13, z_lo, x_o, 1, over)

    def gather_near(h):
        for n in (4, 5, 8, 9):
            gathers[h][n].wait_recv()

    def gather_rest(h):
        for n in (10, 11, 12, 13):
            gathers[h][n].wait_recv()

    def turn(p):
        tile_loads[p].wait()

        def one(i, carry):
            for u in range(8):
                k = p * quarter + i * 8 + u
                tiles[k] = tiles[k].T
            return carry
        lax.fori_loop(0, quarter // 8, one, 0)

    def multiply(h, start, stop, acc):
        def one(g, acc):
            prods, keeps = [], []
            for u in range(GROUP):
                entry = order_ref[g * GROUP + u]
                keeps.append((entry & 1) > 0)
                row = (entry >> 1) & (block_0.shape[0] - 1)
                prods.append(jnp.dot(tiles[entry >> (row_bits + 1)], block[h][row],
                                     preferred_element_type=jnp.float32))
            for u in range(GROUP):
                acc = jnp.where(keeps[u], acc, 0.0) + prods[u]
                runs[g * GROUP + u] = acc.astype(jnp.bfloat16)
            return acc
        return lax.fori_loop(start // GROUP, stop // GROUP, one, acc)

    def chunk(s, d, c):
        z_to = 1 - z_hi if s == 0 else z_hi
        return ((z_to * 4 + lax.rem(y + d, 4)) * 2 + c) * count

    zero = jnp.zeros((LANES, LANES), jnp.bfloat16)
    swaps = ({}, {})

    def swap(h, n):
        s, d = ORDER[n]
        base = chunk(s, d, 1 - core)

        def one(g, carry):
            for u in range(8):
                t = g * 8 + u
                entry = last_ref[base + t]
                mate_part[n, t] = jnp.where((entry & 1) > 0, runs[entry >> 1], zero)
            return carry
        if h == 1:
            swaps[0][n].wait_send()
            done.append(swaps[0][n])
        lax.fori_loop(0, count // 8, one, 0)
        swaps[h][n] = go(2 * GATHER + h * REDUCE + n, mate_part.at[n], core_in.at[h * 8 + s * 4 + d], mate)

    def settle(h, n):
        if n == 0:
            for m in range(3):
                swap(h, m)
        if n + 3 < len(ORDER):
            swap(h, n + 3)
        s, d = ORDER[n]
        base = chunk(s, d, core)
        at = h * 8 + s * 4 + d
        swaps[h][n].wait_recv()

        def one(g, carry):
            for u in range(8):
                t = g * 8 + u
                entry = last_ref[base + t]
                mine_here = jnp.where((entry & 1) > 0, runs[entry >> 1], zero).astype(jnp.float32)
                own[at, t] = (mine_here + core_in[at, t].astype(jnp.float32)).astype(jnp.bfloat16)
            return carry
        lax.fori_loop(0, count // 8, one, 0)

    far, direct, merged, hops = {}, {}, {}, {}

    def base_of(h):
        return 2 * GATHER + h * REDUCE + 8

    def segment(h, g):
        rest = count - FIRST[h]
        s, start, length = ((0, 0, rest), (1, 0, rest), (1, rest, FIRST[h]))[g]
        return s, start, length // 2, h * 8 + s * 4, h * 2 + s

    def spread(h, g):
        s, start, size, at, b = segment(h, g)
        base = base_of(h) + g * 6
        low, high = pl.ds(start, size), pl.ds(start + size, size)
        spot = pl.ds(start // 2, size)
        if g < 2:
            settle(h, s * 4)
        far[h, g] = (go(base, own.at[at + 2, low], far_l.at[b, spot], y_right),
                     go(base + 1, own.at[at + 2, high], far_r.at[b, spot], y_left))
        if g < 2:
            settle(h, s * 4 + 1)
        one = go(base + 2, own.at[at + 1, high], near_l.at[b, high], y_right)
        if g < 2:
            settle(h, s * 4 + 2)
        two = go(base + 3, own.at[at + 3, low], near_r.at[b, low], y_left)
        direct[h, g] = (one, two)
        if g < 2:
            settle(h, s * 4 + 3)

    def add_far(at, start, size, src, b, spot):
        for t in range(size):
            own[at, start + t] = (own[at, start + t].astype(jnp.float32)
                                  + src[b, spot + t].astype(jnp.float32)).astype(jnp.bfloat16)

    def forward(h, g):
        s, start, size, at, b = segment(h, g)
        base = base_of(h) + g * 6
        low, high = pl.ds(start, size), pl.ds(start + size, size)
        far[h, g][0].wait_recv()
        add_far(at + 1, start, size, far_l, b, start // 2)
        one = go(base + 4, own.at[at + 1, low], near_l.at[b, low], y_right)
        far[h, g][1].wait_recv()
        add_far(at + 3, start + size, size, far_r, b, start // 2)
        two = go(base + 5, own.at[at + 3, high], near_r.at[b, high], y_left)
        merged[h, g] = (one, two)

    def near_sum(at, b, t):
        return (own[at, t].astype(jnp.float32) + near_l[b, t].astype(jnp.float32)
                + near_r[b, t].astype(jnp.float32))

    def near_wait(h, g, part):
        merged[h, g][part].wait_recv()
        direct[h, g][1 - part].wait_recv()

    def early_send(h):
        size = FIRST[h] // 2
        for part in range(2):
            rows = pl.ds(count - FIRST[h] + part * size, size)
            hops[h, 4 + part] = go(base_of(h) + 22 + part, own.at[pl.ds(h * 8, 4), rows],
                                   early[h].at[part], below if part else above)

    def early_hop(h):
        for part in range(2):
            hops[h, 4 + part].wait_recv()
            hops[h, 6 + part] = go(base_of(h) + 24 + part, early[h].at[part],
                                   early_in[h].at[part], below if part else above)

    def early_add(h):
        size = FIRST[h] // 2
        for part in range(2):
            hops[h, 6 + part].wait_recv()
            for d in range(4):
                for t in range(size):
                    tt = count - FIRST[h] + part * size + t
                    own[h * 8 + 4 + d, tt] = (
                        own[h * 8 + 4 + d, tt].astype(jnp.float32)
                        + early_in[h][part, d, t].astype(jnp.float32)).astype(jnp.bfloat16)

    def close(h):
        s, start, size, at, b = segment(h, 0)
        for part in range(2):
            near_wait(h, 0, part)

            for t in range(part * size, (part + 1) * size):
                own[at, t] = near_sum(at, b, t).astype(jnp.bfloat16)
            hops[h, part] = go(base_of(h) + 18 + part, own.at[at, pl.ds(part * size, size)],
                               relay.at[h * 2 + part, pl.ds(0, size)], below if part else above)

    def onward(h):
        size = segment(h, 0)[2]
        for part in range(2):
            hops[h, part].wait_recv()
            spot = pl.ds(0, size)
            hops[h, 2 + part] = go(base_of(h) + 20 + part, relay.at[h * 2 + part, spot],
                                   cross.at[h * 2 + part, spot], below if part else above)

    def total_of(h, g):
        s, start, size, at, b = segment(h, g)
        for part in range(2):
            near_wait(h, g, part)
            spot = pl.ds(start + part * size, size)
            total = near_sum(at, b, spot)
            if g == 1:
                hops[h, 2 + part].wait_recv()
                total = total + cross[h * 2 + part, pl.ds(0, size)].astype(jnp.float32)
            summed = total.astype(jnp.bfloat16)
            own[at, spot] = summed
            feats = features[spot].reshape(size * LANES, features.shape[2])
            more = lax.dot_general(feats, summed.reshape(size * LANES, LANES), (((0,), (0,)), ((), ())),
                                   preferred_element_type=jnp.float32)
            column = slice(h * LANES, (h + 1) * LANES)
            held = terms if g == 1 else term
            if part == 0:
                held[:, column] = more
            else:
                held[:, column] += more

    pair = 4

    def feature_grads():
        def one(g, carry):
            spot = pl.ds(g * pair, pair)
            both = jnp.concatenate([own[4, spot].reshape(pair * LANES, LANES),
                                    own[12, spot].reshape(pair * LANES, LANES)], axis=1)
            out = lax.dot_general(both, weight_ref[...], (((1,), (1,)), ((), ())),
                                  preferred_element_type=jnp.float32)
            features[spot] = out.astype(jnp.bfloat16).reshape((pair,) + features.shape[1:])
            return carry
        lax.fori_loop(0, count // pair, one, 0)
        return fetch(9, features, grad_out_hbm)

    nothing = jnp.zeros((LANES, LANES), jnp.float32)
    middle = slots // 2 // GROUP * GROUP
    gather_ring(0)
    gather_over(0)
    mask(1)
    turn(0)
    gather_second(0)
    turn(1)
    turn(2)
    gather_third(0)
    gather_over(1)
    turn(3)
    gather_near(0)
    gather_ring(1)
    gather_rest(0)
    acc = multiply(0, 0, middle, nothing)
    gather_second(1)
    multiply(0, middle, slots, acc)
    spread(0, 0)
    early_send(0)
    early_hop(0)
    gather_third(1)
    forward(0, 0)
    spread(0, 1)
    early_add(0)
    spread(0, 2)
    gather_near(1)
    gather_rest(1)
    close(0)
    forward(0, 1)
    multiply(1, 0, slots, nothing)
    onward(0)
    spread(1, 0)
    early_send(1)
    forward(0, 2)
    forward(1, 0)
    spread(1, 1)
    early_hop(1)
    feature_load.wait()
    total_of(0, 2)
    close(1)
    total_of(0, 1)
    forward(1, 1)
    early_add(1)
    spread(1, 2)
    onward(1)
    forward(1, 2)
    total_of(1, 1)
    total_of(1, 2)
    term[...] = terms[...] + term[...]

    first = 2 * GATHER + 2 * REDUCE
    piece = term.shape[0] // 16
    spot = y * 4 + x

    def piece_of(p):
        return pl.ds(pl.multiple_of(p * piece, piece), piece)

    spots = [lax.rem(y + d // 4, 4) * 4 + lax.rem(x + d % 4, 4) for d in range(1, 16)]
    out = [go(first + d, term.at[piece_of(spots[d - 1])], plane_in.at[d - 1], plane[d - 1])
           for d in range(1, 16)]
    store = feature_grads()
    total = term[piece_of(spot), :]
    for d in range(1, 16):
        out[d - 1].wait_recv()
        total = total + plane_in[d - 1]
    me = z * 2 + core
    z_in[me] = total
    ups = [go(first + 15 + d, z_in.at[me], z_in.at[me], column[d - 1]) for d in range(1, 8)]
    for copy in ups:
        copy.wait_recv()
    total = (((z_in[0] + z_in[1]) + (z_in[2] + z_in[3]))
             + ((z_in[4] + z_in[5]) + (z_in[6] + z_in[7])))
    part = piece_of(spot)
    gw_ref[part, :] = total
    out = [go(first + 22 + d, gw_ref.at[part], gw_ref.at[part], plane[d - 1]) for d in range(1, 16)]
    for copy in out:
        copy.wait_recv()
    store.wait()
    for copy in sent:
        if not any(copy is one for one in done):
            copy.wait_send()


def layer_backward(order, last, grad_out, preact, features, weight, tiles, members):
    count, side, width = grad_out.shape
    depth = weight.shape[0]
    slots = tiles.shape[0]
    piece = (side, LANES)
    full, part = (count,) + piece, (count // 2,) + piece
    n_sems = 2 * GATHER + 2 * REDUCE + SUM

    def bf16(*shape):
        return pltpu.VMEM(shape, jnp.bfloat16)

    def f32(*shape):
        return pltpu.VMEM(shape, jnp.float32)

    return pl.pallas_call(
        layer_kernel,
        name="layer_backward",
        in_specs=[pl.BlockSpec(memory_space=pltpu.SMEM)] * 2
        + [pl.BlockSpec(memory_space=pl.ANY)] * 3
        + [pl.BlockSpec(memory_space=pltpu.VMEM), pl.BlockSpec(memory_space=pl.ANY)],
        out_specs=[pl.BlockSpec(memory_space=pl.ANY), pl.BlockSpec(memory_space=pltpu.VMEM)],
        out_shape=[jax.ShapeDtypeStruct((count, side, width), jnp.bfloat16),
                   jax.ShapeDtypeStruct((depth, width), jnp.float32)],
        scratch_shapes=[
            bf16(slots, *piece),
            bf16(members * count, *piece),
            bf16(members * count, *piece),
            bf16(slots, *piece),
            bf16(8, *full),
            bf16(16, *full),
            bf16(16, *full),
            bf16(4, *part),
            bf16(4, *part),
            bf16(4, *full),
            bf16(4, *full),
            bf16(4, *part),
            bf16(4, *part),
            *[bf16(2, 4, rows // 2, *piece) for rows in FIRST * 2],
            bf16(count, side, width),
            f32(depth, width),
            f32(depth, width),
            f32(15, depth // 16, width),
            f32(8, depth // 16, width),
            pltpu.SemaphoreType.DMA((10,)),
            pltpu.SemaphoreType.DMA((n_sems,)),
            pltpu.SemaphoreType.DMA((n_sems,)),
        ],
        compiler_params=pltpu.CompilerParams(
            collective_id=0, has_side_effects=True, vmem_limit_bytes=63 * 1024 * 1024),
    )(order, last, grad_out, preact, features, weight, tiles)


def result_kernel(a_in, b_in, a_out, b_out):
    a_out[...] = a_in[...]
    b_out[...] = b_in[...]


def results(*arrays):
    return pl.pallas_call(
        result_kernel,
        name="results",
        in_specs=[pl.BlockSpec(memory_space=pltpu.VMEM)] * 2,
        out_specs=[pl.BlockSpec(memory_space=pltpu.VMEM)] * 2,
        out_shape=[jax.ShapeDtypeStruct(a.shape, a.dtype) for a in arrays],
    )(*arrays)


def slot_tables(rows, cols, live_count, row_tiles, col_tiles):
    slots = rows.shape[0]
    k = lax.iota(jnp.int32, slots)
    live = k < live_count
    col = jnp.where(live, cols, col_tiles)
    key = col * slots + k
    rank = jnp.sum((key[None, :] < key[:, None]).astype(jnp.int32), axis=1)
    same = (col[None, :] == col[:, None]) & (k[None, :] < k[:, None])
    again = jnp.max(same.astype(jnp.int32), axis=1)
    packed = (k * row_tiles + rows) * 2 + again
    order = jnp.sum(jnp.where(rank[None, :] == k[:, None], packed[None, :], 0), axis=1)
    c = lax.iota(jnp.int32, col_tiles)
    upto = jnp.sum((col[None, :] <= c[:, None]).astype(jnp.int32), axis=1)
    here = jnp.max((col[None, :] == c[:, None]).astype(jnp.int32), axis=1)
    last = jnp.maximum(upto - 1, 0) * 2 + here
    return order, last


def body(grad_out, preact, features, weight, tiles, tile_rows, tile_cols, live_counts):
    nodes, width = grad_out.shape
    side = tiles.shape[-1]
    slots = tiles.shape[2]
    shape = (nodes // side, side, width)
    members = lax.axis_size("col")
    col_tiles = lax.axis_size("row") * nodes // side
    order, last = slot_tables(
        tile_rows.reshape(slots), tile_cols.reshape(slots), live_counts.reshape(()),
        members * nodes // side, col_tiles)
    grad_features, grad_weight = layer_backward(
        order, last, grad_out.reshape(shape), preact.reshape(shape), features.reshape(shape), weight,
        tiles.reshape(slots, side, side), members)
    return tuple(results(grad_features.reshape(nodes, width), grad_weight))


def solution(mesh):
    in_specs = (
        P(("row", "col"), None),
        P(("row", "col"), None),
        P(("col", "row"), None),
        P(),
        P("row", "col", None, None, None),
        P("row", "col", None),
        P("row", "col", None),
        P("row", "col"),
    )
    out_specs = (P(("col", "row"), None), P())
    return jax.shard_map(body, mesh=mesh, in_specs=in_specs, out_specs=out_specs, check_vma=False)
```
